512 devices in a mesh: fsdp: 64 (over y, x, core), cent: 8 (over z).
Axes of the slice: x: 4, y: 8, z: 8, core: 2. Of those that a mesh axis runs over, the one named last changes fastest.
Arguments:
- attention: bfloat16 [8192, 4096], P('fsdp', 'cent'), may hold values from -6 to 6
- w_out: bfloat16 [4096, 4096], P('cent', 'fsdp'), may hold values from -0.09375 to 0.09375
- hidden: bfloat16 [8192, 4096], P(('fsdp', 'cent')), may hold values from -6 to 6
- norm_gain: bfloat16 [4096], replicated, may hold values from 0.099609375 to 1.8984375
- centroids: bfloat16 [512, 4096], P('cent'), may hold values from -3 to 3
- token_codes: int32 [8192], P(('fsdp', 'cent')), may hold values from 0 to 63, as said below
- tile_lists: int32 [64, 8], P('fsdp'), may hold values from 0 to 63, as said below
Outputs:
- centroid_sums: float32 [512, 4096], P('cent', 'fsdp')
- residual_gram: float32 [4096, 4096], P('fsdp', 'cent')
The draws below stay inside these ranges and needn't reach their ends.
Inputs may be any that keep to these rules, and one draw needn't show every extreme that they name: `token_codes`: token t belongs to block t // 128; its code k names centroid k % 8 of the tile at slot k // 8 of that block's list; every slot of a block's list is used. `tile_lists`: each row holds 8 distinct tile ids in ascending order; tile j holds centroids j * 8 to j * 8 + 7, and centroid g belongs to owner shard g // 64; in every row at most 2 listed tiles share an owner, and exactly 2 do for some owner.
All inputs are finite; a program needn't handle non-finite values.
Results may differ from the reference program's by a relative error of at most 0.0085.
Values may be sent and summed in bfloat16 or wider, within the bound.
A program may use at most 64 MiB of HBM per device.

```python
import jax
import jax.numpy as jnp
from jax import lax

D = 4096
BLOCK = 128
TILE = 8
LT = 8
CAP = 2
CENT_DEV = 64
TOKENS = 8192
NBLOCKS = 64
NCENT = 512
NTILES = 64
N_CENT = 8


def draw_token_codes(key, part):
    rand_keys = jax.random.split(key, 3)
    code_grid = jax.random.randint(rand_keys[0], (NBLOCKS, BLOCK), 0, LT * TILE)
    tile_offsets = jax.random.randint(rand_keys[1], (NBLOCKS, LT), 0, TILE)
    forced = jnp.arange(LT, dtype=jnp.int32)[None, :] * TILE + tile_offsets
    code_grid = code_grid.at[:, :LT].set(forced)
    code_grid = code_grid.at[:, LT].set(0)
    code_grid = code_grid.at[:, LT + 1].set(LT * TILE - 1)
    row_keys = jax.random.split(rand_keys[2], NBLOCKS)
    mixed = jax.vmap(lambda row_key, row: jax.random.permutation(row_key, row))(row_keys, code_grid)
    return mixed.reshape(TOKENS).astype(jnp.int32)


def draw_tile_lists(key, part):
    per_owner = CENT_DEV // TILE
    owners_all = NTILES // per_owner

    def one_block(block_key):
        key_hot, key_perm = jax.random.split(block_key)
        hot_owner = jax.random.randint(key_hot, (), 0, owners_all)
        shuffled = jax.random.permutation(key_perm, NTILES).astype(jnp.int32)
        owner_idx = shuffled // per_owner
        position = jnp.arange(NTILES, dtype=jnp.int32)
        earlier = (owner_idx[None, :] == owner_idx[:, None]) & (position[None, :] < position[:, None])
        owner_rank = jnp.sum(earlier.astype(jnp.int32), axis=1)
        is_hot = owner_idx == hot_owner
        within = owner_rank < CAP
        priority = jnp.where(within, jnp.where(is_hot, position, NTILES + position), 3 * NTILES + position)
        chosen = jnp.argsort(priority)[:LT]
        return jnp.sort(shuffled[chosen])
    return jax.vmap(one_block)(jax.random.split(key, NBLOCKS)).astype(jnp.int32)


def level_of(rng, extent, cuts, least, largest):
    level = 1.0
    for dim, blocks in cuts:
        draws = jax.random.uniform(jax.random.fold_in(jax.random.fold_in(rng, 6), dim), (blocks,), jnp.float32, least / len(cuts), largest / len(cuts))
        level = level * jnp.repeat(jnp.exp(draws), extent[dim] // blocks).reshape((-1,) + (1,) * (len(extent) - 1 - dim))
    return level


def centred(own_key, extent, scale, most, cuts=(), held_as=jnp.bfloat16):
    drawn = jax.random.normal(own_key, extent, jnp.float32) * scale
    if len(cuts) > 0:
        drawn = level_of(own_key, extent, cuts, -0.22, 0.18) * drawn
    return jnp.clip(drawn, min=-most, max=most).astype(held_as)


def setup_inputs(seed: int = 0) -> dict:
    key_of = jax.random.split(jax.random.key(seed), 8)
    attention = centred(key_of[0], (TOKENS, D), 1.0, 6.0, ((0, 64), (1, 8)))
    w_out = centred(key_of[1], (D, D), D ** -0.5, 0.09375, ((0, 8), (1, 64)))
    hidden = centred(key_of[2], (TOKENS, D), 1.0, 6.0, ((0, 512),))
    norm_gain = jnp.clip(1.0 + 0.18 * jax.random.normal(key_of[3], (D,), jnp.float32), 0.099609375, 1.8984375).astype(jnp.bfloat16)
    centroids = centred(key_of[4], (NCENT, D), 0.5, 3.0, ((0, 8),))
    token_codes = draw_token_codes(jax.random.fold_in(key_of[7], 71), 0)
    tile_lists = draw_tile_lists(jax.random.fold_in(key_of[7], 71), 0)
    return {"attention": attention, "w_out": w_out, "hidden": hidden, "norm_gain": norm_gain, "centroids": centroids, "token_codes": token_codes, "tile_lists": tile_lists}


def reference(attention, w_out, hidden, norm_gain, centroids, token_codes, tile_lists):
    feat_block = D // N_CENT
    projected = jnp.zeros((TOKENS, D), jnp.float32)
    for cent_group in range(N_CENT):
        begin_at = cent_group * feat_block
        partial_proj = jnp.dot(attention[:, begin_at:begin_at + feat_block], w_out[begin_at:begin_at + feat_block, :], preferred_element_type=jnp.float32)
        rounded = lax.optimization_barrier(partial_proj.astype(jnp.bfloat16))
        projected = projected + rounded.astype(jnp.float32)
    mixed_rows = hidden.astype(jnp.float32) + projected
    normed = mixed_rows * lax.rsqrt(lax.optimization_barrier(jnp.mean(mixed_rows * mixed_rows, axis=1, keepdims=True)) + 1e-05) * norm_gain.astype(jnp.float32)
    block_of = (jnp.arange(TOKENS) // BLOCK).astype(jnp.int32)
    tile_ids = tile_lists[block_of, token_codes // TILE]
    cent_ids = (tile_ids * TILE + token_codes % TILE).astype(jnp.int32)
    centers = jnp.take(centroids, cent_ids, axis=0).astype(jnp.float32)
    residual = (normed - centers).astype(jnp.bfloat16)
    rows_dev = BLOCK // N_CENT
    grouped = residual.reshape(NBLOCKS * N_CENT, rows_dev, D).astype(jnp.float32)
    grouped_ids = cent_ids.reshape(NBLOCKS * N_CENT, rows_dev)

    def device_part(carry, items):
        rows_here, ids_here = items
        partial_sum = jax.ops.segment_sum(rows_here, ids_here, num_segments=NCENT)
        rounded = lax.optimization_barrier(partial_sum.astype(jnp.bfloat16))
        return (carry + rounded.astype(jnp.float32), None)
    centroid_sums, unused = lax.scan(device_part, jnp.zeros((NCENT, D), jnp.float32), (grouped, grouped_ids))
    residual_gram = jnp.dot(residual.T, residual, preferred_element_type=jnp.float32) / TOKENS
    return (centroid_sums, residual_gram)
```

```python
import functools

import jax
import jax.numpy as jnp
from jax import lax
from jax.experimental import pallas as pl
from jax.experimental.pallas import tpu as pltpu
from jax.sharding import PartitionSpec as P

TILE = 8
LT = 8
MESH = pl.DeviceIdType.MESH


def swap_kernel(n, views, *refs):
    count = len(views)
    sources, landed = refs[:count], refs[count : 2 * count]
    send_sem, recv_sem, own_sem = refs[2 * count :]
    line = lax.axis_index("fsdp")
    me = lax.axis_index("cent")
    barrier = pltpu.get_barrier_semaphore()
    for step in range(1, n):
        pl.semaphore_signal(
            barrier, inc=1, device_id=(line, lax.rem(me + step, n)), device_id_type=MESH
        )
    pl.semaphore_wait(barrier, n - 1)
    copies = []
    for step in sorted(range(1, n), key=lambda s: -min(s, n - s)):
        peer = lax.rem(me + step, n)
        for which in range(count):
            copy = pltpu.make_async_remote_copy(
                src_ref=views[which](sources[which], peer),
                dst_ref=landed[which].at[me],
                send_sem=send_sem.at[which, step],
                recv_sem=recv_sem.at[which, step],
                device_id=(line, peer),
                device_id_type=MESH,
            )
            copy.start()
            copies.append(copy)
    owns = []
    for which in range(count):
        own = pltpu.make_async_copy(
            views[which](sources[which], me), landed[which].at[me], own_sem.at[which]
        )
        own.start()
        owns.append(own)
    for own in owns:
        own.wait()
    for copy in copies:
        copy.wait()


def swap(n, collective_id, operands, views, pieces, work_bytes):
    count = len(operands)
    return pl.pallas_call(
        functools.partial(swap_kernel, n, views),
        out_shape=[
            jax.ShapeDtypeStruct((n,) + piece, operand.dtype)
            for piece, operand in zip(pieces, operands)
        ],
        in_specs=[pl.BlockSpec(memory_space=pltpu.VMEM)] * count,
        out_specs=[pl.BlockSpec(memory_space=pltpu.VMEM)] * count,
        scratch_shapes=[
            pltpu.SemaphoreType.DMA((count, n)),
            pltpu.SemaphoreType.DMA((count, n)),
            pltpu.SemaphoreType.DMA((count,)),
        ],
        compiler_params=pltpu.CompilerParams(collective_id=collective_id, has_side_effects=True),
        cost_estimate=pl.CostEstimate(flops=0, bytes_accessed=work_bytes, transcendentals=0),
    )(*operands)


def whole(ref, peer):
    return ref


def row_piece(ref, peer):
    return ref.at[peer]


def shards(attention, w_out, hidden, norm_gain, centroids, token_codes, tile_lists):
    tok_dev = hidden.shape[0]
    feat_dim = hidden.shape[1]
    n_fsdp = lax.axis_size("fsdp")
    n_cent = lax.axis_size("cent")
    cap_slots = max(2, 2 * LT // n_cent)
    w_cols = lax.all_gather(w_out, "fsdp", axis=1, tiled=True)

    cent_dev = centroids.shape[0]
    own_tiles = cent_dev // TILE
    owner_idx = lax.axis_index("cent")
    listed = tile_lists[0]
    local_tile = listed - owner_idx * own_tiles
    owned_here = (local_tile >= 0) & (local_tile < own_tiles)
    safe_tile = jnp.clip(local_tile, 0, own_tiles - 1)
    tiles_here = centroids.reshape(own_tiles, TILE, feat_dim)
    slot_of = token_codes // TILE
    offset = token_codes % TILE
    list_pos = jnp.arange(LT, dtype=jnp.int32)
    owner_of = listed // own_tiles
    earlier = (owner_of[None, :] == owner_of[:, None]) & (list_pos[None, :] < list_pos[:, None])
    rank_all = jnp.sum(earlier.astype(jnp.int32), axis=1)
    chosen = owned_here[None, :] & (
        rank_all[None, :] == jnp.arange(cap_slots, dtype=jnp.int32)[:, None]
    )
    send_tile = jnp.sum(jnp.where(chosen, safe_tile[None, :], 0), axis=1)
    filled = jnp.any(chosen, axis=1)
    outgoing = jnp.where(
        filled[:, None, None],
        jnp.take(tiles_here, send_tile, axis=0),
        jnp.zeros((cap_slots, TILE, feat_dim), jnp.bfloat16),
    ).reshape(cap_slots * TILE, feat_dim)
    (arrived,) = swap(
        n_cent, 0, [outgoing], [whole], [(cap_slots * TILE, feat_dim)], 64 * 1024 * 1024
    )
    where_tile = owner_of * cap_slots + rank_all
    tile_rows = arrived.reshape(-1, feat_dim)
    centers = jnp.take(tile_rows, where_tile[slot_of] * TILE + offset, axis=0)
    tile_of = listed[slot_of]

    partial_out = jnp.dot(attention, w_cols, preferred_element_type=jnp.float32)
    (parts,) = swap(
        n_cent,
        1,
        [partial_out.astype(jnp.bfloat16).reshape(n_cent, tok_dev, feat_dim)],
        [row_piece],
        [(tok_dev, feat_dim)],
        64 * 1024 * 1024,
    )
    head_sum = jnp.sum(parts.astype(jnp.float32), axis=0)
    mixed_rows = hidden.astype(jnp.float32) + head_sum
    normed = (
        mixed_rows
        * lax.rsqrt(jnp.mean(mixed_rows * mixed_rows, axis=1, keepdims=True) + 1e-05)
        * norm_gain.astype(jnp.float32)
    )
    residual = (normed - centers.astype(jnp.float32)).astype(jnp.bfloat16)

    lane = jnp.arange(128, dtype=jnp.int32)[None, :]
    label = jnp.where(
        lane == 0, tile_of[:, None], jnp.where(lane == 1, offset[:, None], 0)
    ).astype(jnp.bfloat16)
    shard_rows = lax.all_gather(
        jnp.concatenate([residual, label], axis=1), "fsdp", axis=0, tiled=True
    )
    rows_dev = feat_dim // n_fsdp
    row_start = lax.axis_index("fsdp") * rows_dev
    left_cols = lax.dynamic_slice_in_dim(shard_rows, row_start, rows_dev, 1)
    gram_part = lax.dot_general(
        left_cols, shard_rows, (((0,), (0,)), ((), ())), preferred_element_type=jnp.float32
    ).astype(jnp.bfloat16)
    cent_id = (
        shard_rows[:, feat_dim].astype(jnp.float32) * TILE
        + shard_rows[:, feat_dim + 1].astype(jnp.float32)
    ).astype(jnp.int32)
    n_rows = cent_dev * n_cent
    onehot = (cent_id[None, :] == jnp.arange(n_rows, dtype=jnp.int32)[:, None]).astype(
        jnp.bfloat16
    )
    sums_part = jnp.dot(onehot, left_cols, preferred_element_type=jnp.float32)
    cols_dev = feat_dim // n_cent

    def col_piece(ref, peer):
        return ref.at[:, pl.ds(pl.multiple_of(peer * cols_dev, cols_dev), cols_dev)]

    gram_parts, sums_parts = swap(
        n_cent,
        2,
        [gram_part, sums_part.reshape(n_cent, cent_dev, rows_dev)],
        [col_piece, row_piece],
        [(rows_dev, cols_dev), (cent_dev, rows_dev)],
        64 * 1024 * 1024,
    )
    centroid_sums = jnp.sum(sums_parts, axis=0)
    gram_sum = jnp.sum(gram_parts.astype(jnp.float32), axis=0)
    tokens_all = tok_dev * n_fsdp * n_cent
    return (centroid_sums, gram_sum / tokens_all)


def solution(mesh):
    in_specs = (
        P("fsdp", "cent"),
        P("cent", "fsdp"),
        P(("fsdp", "cent"), None),
        P(),
        P("cent", None),
        P(("fsdp", "cent")),
        P("fsdp", None),
    )
    out_specs = (P("cent", "fsdp"), P("fsdp", "cent"))
    return jax.shard_map(shards, mesh=mesh, in_specs=in_specs, out_specs=out_specs, check_vma=False)
```

```python
import functools

import jax
import jax.numpy as jnp
from jax import lax
from jax.experimental import pallas as pl
from jax.experimental.pallas import tpu as pltpu
from jax.sharding import PartitionSpec as P

TILE = 8
LT = 8
NY = 8
NX = 4
MESH = pl.DeviceIdType.MESH


def swap_kernel(n, views, *refs):
    count = len(views)
    sources, landed = refs[:count], refs[count : 2 * count]
    send_sem, recv_sem, own_sem = refs[2 * count :]
    line = lax.axis_index("fsdp")
    me = lax.axis_index("cent")
    barrier = pltpu.get_barrier_semaphore()
    for step in range(1, n):
        pl.semaphore_signal(
            barrier, inc=1, device_id=(line, lax.rem(me + step, n)), device_id_type=MESH
        )
    pl.semaphore_wait(barrier, n - 1)
    copies = []
    for step in sorted(range(1, n), key=lambda s: -min(s, n - s)):
        peer = lax.rem(me + step, n)
        for which in range(count):
            copy = pltpu.make_async_remote_copy(
                src_ref=views[which](sources[which], peer),
                dst_ref=landed[which].at[me],
                send_sem=send_sem.at[which, step],
                recv_sem=recv_sem.at[which, step],
                device_id=(line, peer),
                device_id_type=MESH,
            )
            copy.start()
            copies.append(copy)
    owns = []
    for which in range(count):
        own = pltpu.make_async_copy(
            views[which](sources[which], me), landed[which].at[me], own_sem.at[which]
        )
        own.start()
        owns.append(own)
    for own in owns:
        own.wait()
    for copy in copies:
        copy.wait()


def swap(n, collective_id, operands, views, pieces, work_bytes):
    count = len(operands)
    return pl.pallas_call(
        functools.partial(swap_kernel, n, views),
        out_shape=[
            jax.ShapeDtypeStruct((n,) + piece, operand.dtype)
            for piece, operand in zip(pieces, operands)
        ],
        in_specs=[pl.BlockSpec(memory_space=pltpu.VMEM)] * count,
        out_specs=[pl.BlockSpec(memory_space=pltpu.VMEM)] * count,
        scratch_shapes=[
            pltpu.SemaphoreType.DMA((count, n)),
            pltpu.SemaphoreType.DMA((count, n)),
            pltpu.SemaphoreType.DMA((count,)),
        ],
        compiler_params=pltpu.CompilerParams(collective_id=collective_id, has_side_effects=True),
        cost_estimate=pl.CostEstimate(flops=0, bytes_accessed=work_bytes, transcendentals=0),
    )(*operands)


def ring_arrivals(size, sign):
    arrivals = []
    for hops in range(1, size // 2 + 1):
        arrivals.append((hops, -sign * hops, sign, hops < size // 2))
        if hops < size // 2:
            arrivals.append((hops, sign * hops, -sign, hops < size // 2 - 1))
    return arrivals


def plane_kernel(n_cent, has_tiles, *refs):
    if has_tiles:
        block, tiles, out, tiles_out, send_sem, recv_sem, own_sem, tile_send, tile_recv, tile_own = refs
    else:
        block, out, send_sem, recv_sem, own_sem = refs
    place = lax.axis_index("fsdp")
    me = lax.axis_index("cent")
    my_core = lax.rem(place, 2)
    my_x = lax.rem(place // 2, NX)
    my_y = place // (2 * NX)

    def device_at(dy, dx, core):
        return (lax.rem(my_y + dy + NY, NY) * NX + lax.rem(my_x + dx + NX, NX)) * 2 + core

    barrier = pltpu.get_barrier_semaphore()
    around = [device_at(dy, dx, my_core) for dy, dx in ((1, 0), (-1, 0), (0, 1), (0, -1))]
    around.append(device_at(0, 0, 1 - my_core))
    greeted = len(around)
    for other in around:
        pl.semaphore_signal(barrier, inc=1, device_id=(other, me), device_id_type=MESH)
    if has_tiles:
        greeted += n_cent - 1
        for step in range(1, n_cent):
            pl.semaphore_signal(
                barrier, inc=1, device_id=(place, lax.rem(me + step, n_cent)), device_id_type=MESH
            )
    pl.semaphore_wait(barrier, greeted)

    tile_copies = []
    if has_tiles:
        for step in sorted(range(1, n_cent), key=lambda s: -min(s, n_cent - s)):
            copy = pltpu.make_async_remote_copy(
                src_ref=tiles,
                dst_ref=tiles_out.at[me],
                send_sem=tile_send.at[step],
                recv_sem=tile_recv.at[step],
                device_id=(place, lax.rem(me + step, n_cent)),
                device_id_type=MESH,
            )
            copy.start()
            tile_copies.append(copy)

    def walk(core, first_is_y, sign):
        def offsets(first, second):
            return (first, second) if first_is_y else (second, first)

        sizes = (NY, NX) if first_is_y else (NX, NY)
        copies = []

        def send(source, origin, target):
            copy = pltpu.make_async_remote_copy(
                src_ref=source,
                dst_ref=out.at[origin],
                send_sem=send_sem.at[len(copies)],
                recv_sem=recv_sem.at[origin],
                device_id=(target, me),
                device_id_type=MESH,
            )
            copy.start()
            copies.append(copy)

        def arrive(origin):
            pltpu.make_async_remote_copy(
                src_ref=out.at[origin],
                dst_ref=out.at[origin],
                send_sem=send_sem.at[0],
                recv_sem=recv_sem.at[origin],
                device_id=(device_at(0, 0, 1 - core), me),
                device_id_type=MESH,
            ).wait_recv()

        firsts = [(0, 0, 0, False)] + ring_arrivals(sizes[0], sign)
        seconds = ring_arrivals(sizes[1], sign)
        events = []
        for number, (hops, offset, way, goes_on) in enumerate(firsts):
            events.append((hops, 0, number, 0, (offset, 0), way, goes_on))
            for later, (more, across, turn, on_too) in enumerate(seconds):
                events.append((hops + more, 1, number, later, (offset, across), turn, on_too))
        for hops, leg, unused, also_unused, offset, way, goes_on in sorted(events):
            origin = device_at(*offsets(*offset), core)
            source = block
            if hops > 0:
                arrive(origin)
                source = out.at[origin]
            if leg == 0:
                for turn in (1, -1) if hops == 0 else (way,) if goes_on else ():
                    send(source, origin, device_at(*offsets(turn, 0), core))
                for turn in (1, -1):
                    send(source, origin, device_at(*offsets(0, turn), core))
            elif goes_on:
                send(source, origin, device_at(*offsets(0, way), core))
            send(source, origin, device_at(0, 0, 1 - core))
        own = pltpu.make_async_copy(block, out.at[place], own_sem)
        own.start()
        for chip in range(NY * NX):
            arrive(2 * chip + 1 - core)
        own.wait()
        for copy in copies:
            copy.wait_send()

    @pl.when(my_core == 0)
    def _():
        walk(0, True, 1)

    @pl.when(my_core == 1)
    def _():
        walk(1, False, -1)

    if has_tiles:
        own = pltpu.make_async_copy(tiles, tiles_out.at[me], tile_own)
        own.start()
        own.wait()
        for copy in tile_copies:
            copy.wait()


def plane_gather(n_cent, collective_id, block, tiles=None):
    devices = NY * NX * 2
    operands = [block] if tiles is None else [block, tiles]
    counts = [devices] if tiles is None else [devices, n_cent]
    scratch = [
        pltpu.SemaphoreType.DMA((devices,)),
        pltpu.SemaphoreType.DMA((devices,)),
        pltpu.SemaphoreType.DMA,
    ]
    if tiles is not None:
        scratch += [
            pltpu.SemaphoreType.DMA((n_cent,)),
            pltpu.SemaphoreType.DMA((n_cent,)),
            pltpu.SemaphoreType.DMA,
        ]
    return pl.pallas_call(
        functools.partial(plane_kernel, n_cent, tiles is not None),
        out_shape=[
            jax.ShapeDtypeStruct((count,) + operand.shape, operand.dtype)
            for count, operand in zip(counts, operands)
        ],
        in_specs=[pl.BlockSpec(memory_space=pltpu.VMEM)] * len(operands),
        out_specs=[pl.BlockSpec(memory_space=pltpu.VMEM)] * len(operands),
        scratch_shapes=scratch,
        compiler_params=pltpu.CompilerParams(collective_id=collective_id, has_side_effects=True),
        cost_estimate=pl.CostEstimate(
            flops=0, bytes_accessed=64 * 1024 * 1024, transcendentals=0
        ),
    )(*operands)


def row_piece(ref, peer):
    return ref.at[peer]


def shards(attention, w_out, hidden, norm_gain, centroids, token_codes, tile_lists):
    tok_dev = hidden.shape[0]
    feat_dim = hidden.shape[1]
    n_fsdp = lax.axis_size("fsdp")
    n_cent = lax.axis_size("cent")
    cap_slots = max(2, 2 * LT // n_cent)
    cent_dev = centroids.shape[0]
    own_tiles = cent_dev // TILE
    owner_idx = lax.axis_index("cent")
    listed = tile_lists[0]
    local_tile = listed - owner_idx * own_tiles
    owned_here = (local_tile >= 0) & (local_tile < own_tiles)
    safe_tile = jnp.clip(local_tile, 0, own_tiles - 1)
    tiles_here = centroids.reshape(own_tiles, TILE, feat_dim)
    slot_of = token_codes // TILE
    offset = token_codes % TILE
    list_pos = jnp.arange(LT, dtype=jnp.int32)
    owner_of = listed // own_tiles
    earlier = (owner_of[None, :] == owner_of[:, None]) & (list_pos[None, :] < list_pos[:, None])
    rank_all = jnp.sum(earlier.astype(jnp.int32), axis=1)
    chosen = owned_here[None, :] & (
        rank_all[None, :] == jnp.arange(cap_slots, dtype=jnp.int32)[:, None]
    )
    send_tile = jnp.sum(jnp.where(chosen, safe_tile[None, :], 0), axis=1)
    filled = jnp.any(chosen, axis=1)
    outgoing = jnp.where(
        filled[:, None, None],
        jnp.take(tiles_here, send_tile, axis=0),
        jnp.zeros((cap_slots, TILE, feat_dim), jnp.bfloat16),
    ).reshape(cap_slots * TILE, feat_dim)
    w_rows, arrived = plane_gather(n_cent, 0, w_out.T, outgoing)
    where_tile = owner_of * cap_slots + rank_all
    tile_rows = arrived.reshape(-1, feat_dim)
    centers = jnp.take(tile_rows, where_tile[slot_of] * TILE + offset, axis=0)
    tile_of = listed[slot_of]

    partial_out = lax.dot_general(
        attention,
        w_rows.reshape(feat_dim, attention.shape[1]),
        (((1,), (1,)), ((), ())),
        preferred_element_type=jnp.float32,
    )
    (parts,) = swap(
        n_cent,
        1,
        [partial_out.astype(jnp.bfloat16).reshape(n_cent, tok_dev, feat_dim)],
        [row_piece],
        [(tok_dev, feat_dim)],
        64 * 1024 * 1024,
    )
    head_sum = jnp.sum(parts.astype(jnp.float32), axis=0)
    mixed_rows = hidden.astype(jnp.float32) + head_sum
    normed = (
        mixed_rows
        * lax.rsqrt(jnp.mean(mixed_rows * mixed_rows, axis=1, keepdims=True) + 1e-05)
        * norm_gain.astype(jnp.float32)
    )
    residual = (normed - centers.astype(jnp.float32)).astype(jnp.bfloat16)

    lane = jnp.arange(128, dtype=jnp.int32)[None, :]
    label = jnp.where(
        lane == 0, tile_of[:, None], jnp.where(lane == 1, offset[:, None], 0)
    ).astype(jnp.bfloat16)
    (gathered,) = plane_gather(n_cent, 3, jnp.concatenate([residual, label], axis=1))
    shard_rows = gathered.reshape(-1, gathered.shape[-1])
    rows_dev = feat_dim // n_fsdp
    row_start = lax.axis_index("fsdp") * rows_dev
    left_cols = lax.dynamic_slice_in_dim(shard_rows, row_start, rows_dev, 1)
    gram_part = lax.dot_general(
        left_cols, shard_rows, (((0,), (0,)), ((), ())), preferred_element_type=jnp.float32
    ).astype(jnp.bfloat16)
    cent_id = (
        shard_rows[:, feat_dim].astype(jnp.float32) * TILE
        + shard_rows[:, feat_dim + 1].astype(jnp.float32)
    ).astype(jnp.int32)
    n_rows = cent_dev * n_cent
    onehot = (cent_id[None, :] == jnp.arange(n_rows, dtype=jnp.int32)[:, None]).astype(
        jnp.bfloat16
    )
    sums_part = jnp.dot(onehot, left_cols, preferred_element_type=jnp.float32)
    cols_dev = feat_dim // n_cent

    def col_piece(ref, peer):
        return ref.at[:, pl.ds(pl.multiple_of(peer * cols_dev, cols_dev), cols_dev)]

    gram_parts, sums_parts = swap(
        n_cent,
        2,
        [gram_part, sums_part.reshape(n_cent, cent_dev, rows_dev)],
        [col_piece, row_piece],
        [(rows_dev, cols_dev), (cent_dev, rows_dev)],
        64 * 1024 * 1024,
    )
    centroid_sums = jnp.sum(sums_parts, axis=0)
    gram_sum = jnp.sum(gram_parts.astype(jnp.float32), axis=0)
    tokens_all = tok_dev * n_fsdp * n_cent
    return (centroid_sums, gram_sum / tokens_all)


def solution(mesh):
    in_specs = (
        P("fsdp", "cent"),
        P("cent", "fsdp"),
        P(("fsdp", "cent"), None),
        P(),
        P("cent", None),
        P(("fsdp", "cent")),
        P("fsdp", None),
    )
    out_specs = (P("cent", "fsdp"), P("fsdp", "cent"))
    return jax.shard_map(shards, mesh=mesh, in_specs=in_specs, out_specs=out_specs, check_vma=False)
```

```python
import functools

import jax
import jax.numpy as jnp
from jax import lax
from jax.experimental import pallas as pl
from jax.experimental.pallas import tpu as pltpu
from jax.sharding import PartitionSpec as P

TILE = 8
LT = 8
NY = 8
NX = 4
MESH = pl.DeviceIdType.MESH


def swap_kernel(n, views, *refs):
    count = len(views)
    sources, landed = refs[:count], refs[count : 2 * count]
    send_sem, recv_sem, own_sem, hop_send, hop_recv = refs[2 * count : 2 * count + 5]
    relay = refs[2 * count + 5 :]
    line = lax.axis_index("fsdp")
    me = lax.axis_index("cent")
    my_core = lax.rem(line, 2)
    far, mid = n // 2, n // 4
    barrier = pltpu.get_barrier_semaphore()
    for step in range(1, n):
        pl.semaphore_signal(
            barrier, inc=1, device_id=(line, lax.rem(me + step, n)), device_id_type=MESH
        )
    pl.semaphore_wait(barrier, n - 1)

    def remote(source, target, sent, got, peer):
        return pltpu.make_async_remote_copy(
            src_ref=source,
            dst_ref=target,
            send_sem=sent,
            recv_sem=got,
            device_id=(line, peer),
            device_id_type=MESH,
        )

    def direct(which, step):
        peer = lax.rem(me + step, n)
        return remote(
            views[which](sources[which], peer),
            landed[which].at[me],
            send_sem.at[which, step],
            recv_sem.at[which, step],
            peer,
        )

    def first_hop(which):
        return remote(
            views[which](sources[which], lax.rem(me + far, n)),
            relay[which],
            hop_send.at[which],
            hop_recv.at[which],
            lax.rem(me + n - mid, n),
        )

    def second_hop(which):
        return remote(
            relay[which],
            landed[which].at[lax.rem(me + mid, n)],
            send_sem.at[which, far],
            recv_sem.at[which, far],
            lax.rem(me + n - mid, n),
        )

    @pl.when(my_core == 0)
    def _():
        for which in range(count):
            direct(which, far).start()

    @pl.when(my_core == 1)
    def _():
        for which in range(count):
            first_hop(which).start()

    near = sorted((s for s in range(1, n) if s != far), key=lambda s: -min(s, n - s))
    for step in near:
        for which in range(count):
            direct(which, step).start()
    owns = []
    for which in range(count):
        own = pltpu.make_async_copy(
            views[which](sources[which], me), landed[which].at[me], own_sem.at[which]
        )
        own.start()
        owns.append(own)

    @pl.when(my_core == 1)
    def _():
        for which in range(count):
            first_hop(which).wait()
            second_hop(which).start()

    for own in owns:
        own.wait()
    for step in near:
        for which in range(count):
            direct(which, step).wait()

    @pl.when(my_core == 0)
    def _():
        for which in range(count):
            direct(which, far).wait()

    @pl.when(my_core == 1)
    def _():
        for which in range(count):
            second_hop(which).wait()


def swap(n, collective_id, operands, views, pieces, work_bytes):
    count = len(operands)
    return pl.pallas_call(
        functools.partial(swap_kernel, n, views),
        out_shape=[
            jax.ShapeDtypeStruct((n,) + piece, operand.dtype)
            for piece, operand in zip(pieces, operands)
        ],
        in_specs=[pl.BlockSpec(memory_space=pltpu.VMEM)] * count,
        out_specs=[pl.BlockSpec(memory_space=pltpu.VMEM)] * count,
        scratch_shapes=[
            pltpu.SemaphoreType.DMA((count, n)),
            pltpu.SemaphoreType.DMA((count, n)),
            pltpu.SemaphoreType.DMA((count,)),
            pltpu.SemaphoreType.DMA((count,)),
            pltpu.SemaphoreType.DMA((count,)),
        ]
        + [pltpu.VMEM(piece, operand.dtype) for piece, operand in zip(pieces, operands)],
        compiler_params=pltpu.CompilerParams(collective_id=collective_id, has_side_effects=True),
        cost_estimate=pl.CostEstimate(flops=0, bytes_accessed=work_bytes, transcendentals=0),
    )(*operands)


def ring_arrivals(size, sign):
    arrivals = []
    for hops in range(1, size // 2 + 1):
        arrivals.append((hops, -sign * hops, sign, hops < size // 2))
        if hops < size // 2:
            arrivals.append((hops, sign * hops, -sign, hops < size // 2 - 1))
    return arrivals


def plane_kernel(n_cent, has_tiles, *refs):
    if has_tiles:
        block, tiles, out, tiles_out, send_sem, recv_sem, own_sem, tile_send, tile_recv, tile_own = refs
    else:
        block, out, send_sem, recv_sem, own_sem = refs
    place = lax.axis_index("fsdp")
    me = lax.axis_index("cent")
    my_core = lax.rem(place, 2)
    my_x = lax.rem(place // 2, NX)
    my_y = place // (2 * NX)

    def device_at(dy, dx, core):
        return (lax.rem(my_y + dy + NY, NY) * NX + lax.rem(my_x + dx + NX, NX)) * 2 + core

    barrier = pltpu.get_barrier_semaphore()
    around = [device_at(dy, dx, my_core) for dy, dx in ((1, 0), (-1, 0), (0, 1), (0, -1))]
    around.append(device_at(0, 0, 1 - my_core))
    greeted = len(around)
    for other in around:
        pl.semaphore_signal(barrier, inc=1, device_id=(other, me), device_id_type=MESH)
    if has_tiles:
        greeted += n_cent - 1
        for step in range(1, n_cent):
            pl.semaphore_signal(
                barrier, inc=1, device_id=(place, lax.rem(me + step, n_cent)), device_id_type=MESH
            )
    pl.semaphore_wait(barrier, greeted)

    tile_copies = []
    if has_tiles:
        for step in sorted(range(1, n_cent), key=lambda s: -min(s, n_cent - s)):
            copy = pltpu.make_async_remote_copy(
                src_ref=tiles,
                dst_ref=tiles_out.at[me],
                send_sem=tile_send.at[step],
                recv_sem=tile_recv.at[step],
                device_id=(place, lax.rem(me + step, n_cent)),
                device_id_type=MESH,
            )
            copy.start()
            tile_copies.append(copy)

    def walk(core, first_is_y, sign):
        def offsets(first, second):
            return (first, second) if first_is_y else (second, first)

        sizes = (NY, NX) if first_is_y else (NX, NY)
        copies = []

        def send(source, origin, target):
            copy = pltpu.make_async_remote_copy(
                src_ref=source,
                dst_ref=out.at[origin],
                send_sem=send_sem.at[len(copies)],
                recv_sem=recv_sem.at[origin],
                device_id=(target, me),
                device_id_type=MESH,
            )
            copy.start()
            copies.append(copy)

        def arrive(origin):
            pltpu.make_async_remote_copy(
                src_ref=out.at[origin],
                dst_ref=out.at[origin],
                send_sem=send_sem.at[0],
                recv_sem=recv_sem.at[origin],
                device_id=(device_at(0, 0, 1 - core), me),
                device_id_type=MESH,
            ).wait_recv()

        firsts = [(0, 0, 0, False)] + ring_arrivals(sizes[0], sign)
        seconds = ring_arrivals(sizes[1], sign)
        events = []
        for number, (hops, offset, way, goes_on) in enumerate(firsts):
            events.append((hops, 0, number, 0, (offset, 0), way, goes_on))
            for later, (more, across, turn, on_too) in enumerate(seconds):
                events.append((hops + more, 1, number, later, (offset, across), turn, on_too))
        for hops, leg, unused, also_unused, offset, way, goes_on in sorted(events):
            origin = device_at(*offsets(*offset), core)
            source = block
            if hops > 0:
                arrive(origin)
                source = out.at[origin]
            if leg == 0:
                for turn in (1, -1) if hops == 0 else (way,) if goes_on else ():
                    send(source, origin, device_at(*offsets(turn, 0), core))
                for turn in (1, -1):
                    send(source, origin, device_at(*offsets(0, turn), core))
            elif goes_on:
                send(source, origin, device_at(*offsets(0, way), core))
            send(source, origin, device_at(0, 0, 1 - core))
        own = pltpu.make_async_copy(block, out.at[place], own_sem)
        own.start()
        for chip in range(NY * NX):
            arrive(2 * chip + 1 - core)
        own.wait()
        for copy in copies:
            copy.wait_send()

    @pl.when(my_core == 0)
    def _():
        walk(0, True, 1)

    @pl.when(my_core == 1)
    def _():
        walk(1, False, -1)

    if has_tiles:
        own = pltpu.make_async_copy(tiles, tiles_out.at[me], tile_own)
        own.start()
        own.wait()
        for copy in tile_copies:
            copy.wait()


def plane_gather(n_cent, collective_id, block, tiles=None):
    devices = NY * NX * 2
    operands = [block] if tiles is None else [block, tiles]
    counts = [devices] if tiles is None else [devices, n_cent]
    scratch = [
        pltpu.SemaphoreType.DMA((devices,)),
        pltpu.SemaphoreType.DMA((devices,)),
        pltpu.SemaphoreType.DMA,
    ]
    if tiles is not None:
        scratch += [
            pltpu.SemaphoreType.DMA((n_cent,)),
            pltpu.SemaphoreType.DMA((n_cent,)),
            pltpu.SemaphoreType.DMA,
        ]
    return pl.pallas_call(
        functools.partial(plane_kernel, n_cent, tiles is not None),
        out_shape=[
            jax.ShapeDtypeStruct((count,) + operand.shape, operand.dtype)
            for count, operand in zip(counts, operands)
        ],
        in_specs=[pl.BlockSpec(memory_space=pltpu.VMEM)] * len(operands),
        out_specs=[pl.BlockSpec(memory_space=pltpu.VMEM)] * len(operands),
        scratch_shapes=scratch,
        compiler_params=pltpu.CompilerParams(collective_id=collective_id, has_side_effects=True),
        cost_estimate=pl.CostEstimate(
            flops=0, bytes_accessed=64 * 1024 * 1024, transcendentals=0
        ),
    )(*operands)


def row_piece(ref, peer):
    return ref.at[peer]


def shards(attention, w_out, hidden, norm_gain, centroids, token_codes, tile_lists):
    tok_dev = hidden.shape[0]
    feat_dim = hidden.shape[1]
    n_fsdp = lax.axis_size("fsdp")
    n_cent = lax.axis_size("cent")
    cap_slots = max(2, 2 * LT // n_cent)
    cent_dev = centroids.shape[0]
    own_tiles = cent_dev // TILE
    owner_idx = lax.axis_index("cent")
    listed = tile_lists[0]
    local_tile = listed - owner_idx * own_tiles
    owned_here = (local_tile >= 0) & (local_tile < own_tiles)
    safe_tile = jnp.clip(local_tile, 0, own_tiles - 1)
    tiles_here = centroids.reshape(own_tiles, TILE, feat_dim)
    slot_of = token_codes // TILE
    offset = token_codes % TILE
    list_pos = jnp.arange(LT, dtype=jnp.int32)
    owner_of = listed // own_tiles
    earlier = (owner_of[None, :] == owner_of[:, None]) & (list_pos[None, :] < list_pos[:, None])
    rank_all = jnp.sum(earlier.astype(jnp.int32), axis=1)
    chosen = owned_here[None, :] & (
        rank_all[None, :] == jnp.arange(cap_slots, dtype=jnp.int32)[:, None]
    )
    send_tile = jnp.sum(jnp.where(chosen, safe_tile[None, :], 0), axis=1)
    outgoing = jnp.take(tiles_here, send_tile, axis=0).reshape(cap_slots * TILE, feat_dim)
    w_rows, arrived = plane_gather(n_cent, 0, w_out.T, outgoing)
    where_tile = owner_of * cap_slots + rank_all
    tile_rows = arrived.reshape(-1, feat_dim)
    centers = jnp.take(tile_rows, where_tile[slot_of] * TILE + offset, axis=0)
    tile_of = listed[slot_of]

    partial_out = lax.dot_general(
        attention,
        w_rows.reshape(feat_dim, attention.shape[1]),
        (((1,), (1,)), ((), ())),
        preferred_element_type=jnp.float32,
    )
    (parts,) = swap(
        n_cent,
        1,
        [partial_out.astype(jnp.bfloat16).reshape(n_cent, tok_dev, feat_dim)],
        [row_piece],
        [(tok_dev, feat_dim)],
        64 * 1024 * 1024,
    )
    head_sum = jnp.sum(parts.astype(jnp.float32), axis=0)
    mixed_rows = hidden.astype(jnp.float32) + head_sum
    normed = (
        mixed_rows
        * lax.rsqrt(jnp.mean(mixed_rows * mixed_rows, axis=1, keepdims=True) + 1e-05)
        * norm_gain.astype(jnp.float32)
    )
    residual = (normed - centers.astype(jnp.float32)).astype(jnp.bfloat16)

    lane = jnp.arange(128, dtype=jnp.int32)[None, :]
    label = jnp.where(
        lane == 0, tile_of[:, None], jnp.where(lane == 1, offset[:, None], 0)
    ).astype(jnp.bfloat16)
    (gathered,) = plane_gather(n_cent, 3, jnp.concatenate([residual, label], axis=1))
    shard_rows = gathered.reshape(-1, gathered.shape[-1])
    rows_dev = feat_dim // n_fsdp
    row_start = lax.axis_index("fsdp") * rows_dev
    left_cols = lax.dynamic_slice_in_dim(shard_rows, row_start, rows_dev, 1)
    gram_part = lax.dot_general(
        left_cols, shard_rows, (((0,), (0,)), ((), ())), preferred_element_type=jnp.float32
    ).astype(jnp.bfloat16)
    cent_id = (
        shard_rows[:, feat_dim].astype(jnp.float32) * TILE
        + shard_rows[:, feat_dim + 1].astype(jnp.float32)
    ).astype(jnp.int32)
    n_rows = cent_dev * n_cent
    onehot = (cent_id[None, :] == jnp.arange(n_rows, dtype=jnp.int32)[:, None]).astype(
        jnp.bfloat16
    )
    sums_part = jnp.dot(onehot, left_cols, preferred_element_type=jnp.float32).astype(jnp.bfloat16)
    cols_dev = feat_dim // n_cent

    def col_piece(ref, peer):
        return ref.at[:, pl.ds(pl.multiple_of(peer * cols_dev, cols_dev), cols_dev)]

    gram_parts, sums_parts = swap(
        n_cent,
        2,
        [gram_part, sums_part.reshape(n_cent, cent_dev, rows_dev)],
        [col_piece, row_piece],
        [(rows_dev, cols_dev), (cent_dev, rows_dev)],
        64 * 1024 * 1024,
    )
    centroid_sums = jnp.sum(sums_parts.astype(jnp.float32), axis=0)
    gram_sum = jnp.sum(gram_parts.astype(jnp.float32), axis=0)
    tokens_all = tok_dev * n_fsdp * n_cent
    return (centroid_sums, gram_sum / tokens_all)


def solution(mesh):
    in_specs = (
        P("fsdp", "cent"),
        P("cent", "fsdp"),
        P(("fsdp", "cent"), None),
        P(),
        P("cent", None),
        P(("fsdp", "cent")),
        P("fsdp", None),
    )
    out_specs = (P("cent", "fsdp"), P("fsdp", "cent"))
    return jax.shard_map(shards, mesh=mesh, in_specs=in_specs, out_specs=out_specs, check_vma=False)
```

```python
import functools

import jax
import jax.numpy as jnp
from jax import lax
from jax.experimental import pallas as pl
from jax.experimental.pallas import tpu as pltpu
from jax.sharding import PartitionSpec as P

TILE = 8
LT = 8
NY = 8
NX = 4
MESH = pl.DeviceIdType.MESH


def swap_kernel(n, views, *refs):
    count = len(views)
    sources, landed = refs[:count], refs[count : 2 * count]
    send_sem, recv_sem, own_sem, hop_send, hop_recv = refs[2 * count : 2 * count + 5]
    relay = refs[2 * count + 5 :]
    line = lax.axis_index("fsdp")
    me = lax.axis_index("cent")
    my_core = lax.rem(line, 2)
    far, mid = n // 2, n // 4
    barrier = pltpu.get_barrier_semaphore()
    for step in range(1, n):
        pl.semaphore_signal(
            barrier, inc=1, device_id=(line, lax.rem(me + step, n)), device_id_type=MESH
        )
    pl.semaphore_wait(barrier, n - 1)

    def remote(source, target, sent, got, peer):
        return pltpu.make_async_remote_copy(
            src_ref=source,
            dst_ref=target,
            send_sem=sent,
            recv_sem=got,
            device_id=(line, peer),
            device_id_type=MESH,
        )

    def direct(which, step):
        peer = lax.rem(me + step, n)
        return remote(
            views[which](sources[which], peer),
            landed[which].at[me],
            send_sem.at[which, step],
            recv_sem.at[which, step],
            peer,
        )

    def first_hop(which):
        return remote(
            views[which](sources[which], lax.rem(me + far, n)),
            relay[which],
            hop_send.at[which],
            hop_recv.at[which],
            lax.rem(me + n - mid, n),
        )

    def second_hop(which):
        return remote(
            relay[which],
            landed[which].at[lax.rem(me + mid, n)],
            send_sem.at[which, far],
            recv_sem.at[which, far],
            lax.rem(me + n - mid, n),
        )

    @pl.when(my_core == 0)
    def _():
        for which in range(count):
            direct(which, far).start()

    @pl.when(my_core == 1)
    def _():
        for which in range(count):
            first_hop(which).start()

    near = sorted((s for s in range(1, n) if s != far), key=lambda s: -min(s, n - s))
    for step in near:
        for which in range(count):
            direct(which, step).start()
    owns = []
    for which in range(count):
        own = pltpu.make_async_copy(
            views[which](sources[which], me), landed[which].at[me], own_sem.at[which]
        )
        own.start()
        owns.append(own)

    @pl.when(my_core == 1)
    def _():
        for which in range(count):
            first_hop(which).wait()
            second_hop(which).start()

    for own in owns:
        own.wait()
    for step in near:
        for which in range(count):
            direct(which, step).wait()

    @pl.when(my_core == 0)
    def _():
        for which in range(count):
            direct(which, far).wait()

    @pl.when(my_core == 1)
    def _():
        for which in range(count):
            second_hop(which).wait()


def swap(n, collective_id, operands, views, pieces, work_bytes):
    count = len(operands)
    return pl.pallas_call(
        functools.partial(swap_kernel, n, views),
        out_shape=[
            jax.ShapeDtypeStruct((n,) + piece, operand.dtype)
            for piece, operand in zip(pieces, operands)
        ],
        in_specs=[pl.BlockSpec(memory_space=pltpu.VMEM)] * count,
        out_specs=[pl.BlockSpec(memory_space=pltpu.VMEM)] * count,
        scratch_shapes=[
            pltpu.SemaphoreType.DMA((count, n)),
            pltpu.SemaphoreType.DMA((count, n)),
            pltpu.SemaphoreType.DMA((count,)),
            pltpu.SemaphoreType.DMA((count,)),
            pltpu.SemaphoreType.DMA((count,)),
        ]
        + [pltpu.VMEM(piece, operand.dtype) for piece, operand in zip(pieces, operands)],
        compiler_params=pltpu.CompilerParams(collective_id=collective_id, has_side_effects=True),
        cost_estimate=pl.CostEstimate(flops=0, bytes_accessed=work_bytes, transcendentals=0),
    )(*operands)


def ring_arrivals(size, sign):
    arrivals = []
    for hops in range(1, size // 2 + 1):
        arrivals.append((hops, -sign * hops, sign, hops < size // 2))
        if hops < size // 2:
            arrivals.append((hops, sign * hops, -sign, hops < size // 2 - 1))
    return arrivals


def chip_order():
    def hops(chip):
        return min(chip[0], NY - chip[0]) + min(chip[1], NX - chip[1])

    return sorted(((dy, dx) for dy in range(NY) for dx in range(NX)), key=lambda c: (hops(c), c))


def plane_device(place, dy, dx, core):
    x = lax.rem(place // 2, NX)
    y = place // (2 * NX)
    return (lax.rem(y + dy + NY, NY) * NX + lax.rem(x + dx + NX, NX)) * 2 + core


def greet(place, me, peers):
    my_core = lax.rem(place, 2)
    barrier = pltpu.get_barrier_semaphore()
    around = [plane_device(place, dy, dx, my_core) for dy, dx in ((1, 0), (-1, 0), (0, 1), (0, -1))]
    around.append(plane_device(place, 0, 0, 1 - my_core))
    for other in around:
        pl.semaphore_signal(barrier, inc=1, device_id=(other, me), device_id_type=MESH)
    for peer in peers:
        pl.semaphore_signal(barrier, inc=1, device_id=(place, peer), device_id_type=MESH)
    pl.semaphore_wait(barrier, len(around) + len(peers))


def plane_walk(core, place, me, block, out, send_sem, recv_sem, own_sem, after=None):
    first_is_y, sign = core == 0, 1 - 2 * core

    def offsets(first, second):
        return (first, second) if first_is_y else (second, first)

    def device_at(dy, dx, which):
        return plane_device(place, dy, dx, which)

    sizes = (NY, NX) if first_is_y else (NX, NY)
    copies = []
    here = {(0, 0, core)}

    def send(source, origin, target):
        copy = pltpu.make_async_remote_copy(
            src_ref=source,
            dst_ref=out.at[origin],
            send_sem=send_sem.at[len(copies)],
            recv_sem=recv_sem.at[origin],
            device_id=(target, me),
            device_id_type=MESH,
        )
        copy.start()
        copies.append(copy)

    def arrive(dy, dx, which):
        if (dy % NY, dx % NX, which) in here:
            return
        here.add((dy % NY, dx % NX, which))
        origin = device_at(dy, dx, which)
        pltpu.make_async_remote_copy(
            src_ref=out.at[origin],
            dst_ref=out.at[origin],
            send_sem=send_sem.at[0],
            recv_sem=recv_sem.at[origin],
            device_id=(device_at(0, 0, 1 - core), me),
            device_id_type=MESH,
        ).wait_recv()

    own = pltpu.make_async_copy(block, out.at[place], own_sem)
    own.start()
    firsts = [(0, 0, 0, False)] + ring_arrivals(sizes[0], sign)
    seconds = ring_arrivals(sizes[1], sign)
    events = []
    for number, (hops, offset, way, goes_on) in enumerate(firsts):
        events.append((hops, 0, number, 0, (offset, 0), way, goes_on))
        for later, (more, across, turn, on_too) in enumerate(seconds):
            events.append((hops + more, 1, number, later, (offset, across), turn, on_too))
    events.sort()
    for at, (hops, leg, unused, also_unused, offset, way, goes_on) in enumerate(events):
        dy, dx = offsets(*offset)
        origin = device_at(dy, dx, core)
        source = block
        if hops > 0:
            arrive(dy, dx, core)
            source = out.at[origin]
        if leg == 0:
            for turn in (1, -1) if hops == 0 else (way,) if goes_on else ():
                send(source, origin, device_at(*offsets(turn, 0), core))
            for turn in (1, -1):
                send(source, origin, device_at(*offsets(0, turn), core))
        elif goes_on:
            send(source, origin, device_at(*offsets(0, way), core))
        send(source, origin, device_at(0, 0, 1 - core))
        if at + 1 == len(events) or events[at + 1][0] > hops:
            if hops == 0:
                own.wait()
            if after is not None:
                after(hops, arrive)
    for dy, dx in chip_order():
        arrive(dy, dx, 1 - core)
    for copy in copies:
        copy.wait_send()


def plane_kernel(block, out, send_sem, recv_sem, own_sem):
    place, me = lax.axis_index("fsdp"), lax.axis_index("cent")
    greet(place, me, [])
    for core in range(2):

        @pl.when(lax.rem(place, 2) == core)
        def _():
            plane_walk(core, place, me, block, out, send_sem, recv_sem, own_sem)


def plane_gather(collective_id, block):
    devices = NY * NX * 2
    return pl.pallas_call(
        plane_kernel,
        out_shape=jax.ShapeDtypeStruct((devices,) + block.shape, block.dtype),
        in_specs=[pl.BlockSpec(memory_space=pltpu.VMEM)],
        out_specs=pl.BlockSpec(memory_space=pltpu.VMEM),
        scratch_shapes=[
            pltpu.SemaphoreType.DMA((devices,)),
            pltpu.SemaphoreType.DMA((devices,)),
            pltpu.SemaphoreType.DMA,
        ],
        compiler_params=pltpu.CompilerParams(collective_id=collective_id, has_side_effects=True),
    )(block)


GROUPS = 4


def project_kernel(n, *refs):
    attention, block, tiles, head, tiles_out = refs[:5]
    w_all, stage, landed, send_sem, recv_sem, own_sem, part_send, part_recv = refs[5:13]
    tile_send, tile_recv, tile_own = refs[13:]
    place, me = lax.axis_index("fsdp"), lax.axis_index("cent")
    greet(place, me, [lax.rem(me + step, n) for step in range(1, n)])
    order = chip_order()
    per_group = len(order) // GROUPS
    tok_dev = head.shape[0]

    def part(group, step):
        peer = lax.rem(me + step, n)
        slots = pl.ds(group * per_group, per_group)
        return pltpu.make_async_remote_copy(
            src_ref=stage.at[peer, slots],
            dst_ref=landed.at[step, slots],
            send_sem=part_send.at[group, step],
            recv_sem=part_recv.at[group, step],
            device_id=(place, peer),
            device_id_type=MESH,
        )

    def tile(source, origin, offset, way):
        return pltpu.make_async_remote_copy(
            src_ref=source,
            dst_ref=tiles_out.at[origin],
            send_sem=tile_send.at[(offset - way) % n],
            recv_sem=tile_recv.at[(offset - way) % n],
            device_id=(place, lax.rem(me + way + n, n)),
            device_id_type=MESH,
        )

    def run(core):
        turns = ring_arrivals(n, 1 - 2 * core) if n > 2 else [(1, 1, -1, False)]
        sent = []

        def pass_tiles(hops):
            if hops == 0:
                for way in (1, -1) if n > 2 else (1,):
                    copy = tile(tiles, me, 0, way)
                    copy.start()
                    sent.append(copy)
            for steps, offset, way, goes_on in turns:
                if steps == hops:
                    origin = lax.rem(me + offset + n, n)
                    tile(tiles_out.at[origin], origin, offset + way, way).wait_recv()
                    if goes_on:
                        copy = tile(tiles_out.at[origin], origin, offset, way)
                        copy.start()
                        sent.append(copy)

        def multiply(group, arrive):
            rows = attention[...]
            for slot in range(group * per_group, (group + 1) * per_group):
                dy, dx = order[slot]
                arrive(dy, dx, 0)
                arrive(dy, dx, 1)
                both = w_all[pl.ds(plane_device(place, dy, dx, 0), 2)]
                columns = lax.dot_general(
                    rows,
                    both.reshape(2 * both.shape[1], both.shape[2]),
                    (((1,), (1,)), ((), ())),
                    preferred_element_type=jnp.float32,
                ).astype(jnp.bfloat16)
                stage[:, slot] = columns.reshape(n, tok_dev, columns.shape[1])
            for step in sorted(range(1, n), key=lambda s: -min(s, n - s)):
                part(group, step).start()

        def after(hops, arrive):
            pass_tiles(hops)
            if 3 <= hops <= 5:
                multiply(hops - 3, arrive)
            elif hops == 6:
                multiply(3, arrive)

        plane_walk(core, place, me, block, w_all, send_sem, recv_sem, own_sem, after)
        for copy in sent:
            copy.wait_send()

    for core in range(2):

        @pl.when(lax.rem(place, 2) == core)
        def _():
            run(core)

    own = pltpu.make_async_copy(tiles, tiles_out.at[me], tile_own)
    own.start()
    for group in range(GROUPS):
        for step in range(1, n):
            part(group, step).wait()
        for slot in range(group * per_group, (group + 1) * per_group):
            total = stage[me, slot].astype(jnp.float32)
            for step in range(1, n):
                total = total + landed[step, slot].astype(jnp.float32)
            dy, dx = order[slot]
            start = pl.multiple_of(plane_device(place, dy, dx, 0) // 2 * 128, 128)
            head[:, pl.ds(start, 128)] = total
    own.wait()


def project(n, collective_id, attention, block, tiles):
    devices = NY * NX * 2
    tok_dev = attention.shape[0] // n
    chips = NY * NX
    wide = 2 * block.shape[0]
    pieces = pltpu.VMEM((n, chips, tok_dev, wide), jnp.bfloat16)
    return pl.pallas_call(
        functools.partial(project_kernel, n),
        out_shape=[
            jax.ShapeDtypeStruct((tok_dev, chips * wide), jnp.float32),
            jax.ShapeDtypeStruct((n,) + tiles.shape, tiles.dtype),
        ],
        in_specs=[pl.BlockSpec(memory_space=pltpu.VMEM)] * 3,
        out_specs=[pl.BlockSpec(memory_space=pltpu.VMEM)] * 2,
        scratch_shapes=[
            pltpu.VMEM((devices,) + block.shape, block.dtype),
            pieces,
            pieces,
            pltpu.SemaphoreType.DMA((devices,)),
            pltpu.SemaphoreType.DMA((devices,)),
            pltpu.SemaphoreType.DMA,
            pltpu.SemaphoreType.DMA((GROUPS, n)),
            pltpu.SemaphoreType.DMA((GROUPS, n)),
            pltpu.SemaphoreType.DMA((n,)),
            pltpu.SemaphoreType.DMA((n,)),
            pltpu.SemaphoreType.DMA,
        ],
        compiler_params=pltpu.CompilerParams(
            collective_id=collective_id, has_side_effects=True, vmem_limit_bytes=32 * 1024 * 1024
        ),
    )(attention, block, tiles)


def row_piece(ref, peer):
    return ref.at[peer]


def shards(attention, w_out, hidden, norm_gain, centroids, token_codes, tile_lists):
    tok_dev = hidden.shape[0]
    feat_dim = hidden.shape[1]
    n_fsdp = lax.axis_size("fsdp")
    n_cent = lax.axis_size("cent")
    cap_slots = max(2, 2 * LT // n_cent)
    cent_dev = centroids.shape[0]
    own_tiles = cent_dev // TILE
    owner_idx = lax.axis_index("cent")
    listed = tile_lists[0]
    local_tile = listed - owner_idx * own_tiles
    owned_here = (local_tile >= 0) & (local_tile < own_tiles)
    safe_tile = jnp.clip(local_tile, 0, own_tiles - 1)
    tiles_here = centroids.reshape(own_tiles, TILE, feat_dim)
    slot_of = token_codes // TILE
    offset = token_codes % TILE
    list_pos = jnp.arange(LT, dtype=jnp.int32)
    owner_of = listed // own_tiles
    earlier = (owner_of[None, :] == owner_of[:, None]) & (list_pos[None, :] < list_pos[:, None])
    rank_all = jnp.sum(earlier.astype(jnp.int32), axis=1)
    chosen = owned_here[None, :] & (
        rank_all[None, :] == jnp.arange(cap_slots, dtype=jnp.int32)[:, None]
    )
    send_tile = jnp.sum(jnp.where(chosen, safe_tile[None, :], 0), axis=1)
    outgoing = jnp.take(tiles_here, send_tile, axis=0).reshape(cap_slots * TILE, feat_dim)
    head_sum, arrived = project(n_cent, 0, attention, w_out.T, outgoing)
    where_tile = owner_of * cap_slots + rank_all
    tile_rows = arrived.reshape(-1, feat_dim)
    centers = jnp.take(tile_rows, where_tile[slot_of] * TILE + offset, axis=0)
    tile_of = listed[slot_of]

    mixed_rows = hidden.astype(jnp.float32) + head_sum
    normed = (
        mixed_rows
        * lax.rsqrt(jnp.mean(mixed_rows * mixed_rows, axis=1, keepdims=True) + 1e-05)
        * norm_gain.astype(jnp.float32)
    )
    residual = (normed - centers.astype(jnp.float32)).astype(jnp.bfloat16)

    lane = jnp.arange(128, dtype=jnp.int32)[None, :]
    label = jnp.where(
        lane == 0, tile_of[:, None], jnp.where(lane == 1, offset[:, None], 0)
    ).astype(jnp.bfloat16)
    gathered = plane_gather(3, jnp.concatenate([residual, label], axis=1))
    shard_rows = gathered.reshape(-1, gathered.shape[-1])
    rows_dev = feat_dim // n_fsdp
    row_start = lax.axis_index("fsdp") * rows_dev
    left_cols = lax.dynamic_slice_in_dim(shard_rows, row_start, rows_dev, 1)
    gram_part = lax.dot_general(
        left_cols, shard_rows, (((0,), (0,)), ((), ())), preferred_element_type=jnp.float32
    ).astype(jnp.bfloat16)
    cent_id = (
        shard_rows[:, feat_dim].astype(jnp.float32) * TILE
        + shard_rows[:, feat_dim + 1].astype(jnp.float32)
    ).astype(jnp.int32)
    n_rows = cent_dev * n_cent
    onehot = (cent_id[None, :] == jnp.arange(n_rows, dtype=jnp.int32)[:, None]).astype(
        jnp.bfloat16
    )
    sums_part = jnp.dot(onehot, left_cols, preferred_element_type=jnp.float32).astype(jnp.bfloat16)
    cols_dev = feat_dim // n_cent

    def col_piece(ref, peer):
        return ref.at[:, pl.ds(pl.multiple_of(peer * cols_dev, cols_dev), cols_dev)]

    gram_parts, sums_parts = swap(
        n_cent,
        2,
        [gram_part, sums_part.reshape(n_cent, cent_dev, rows_dev)],
        [col_piece, row_piece],
        [(rows_dev, cols_dev), (cent_dev, rows_dev)],
        64 * 1024 * 1024,
    )
    centroid_sums = jnp.sum(sums_parts.astype(jnp.float32), axis=0)
    gram_sum = jnp.sum(gram_parts.astype(jnp.float32), axis=0)
    tokens_all = tok_dev * n_fsdp * n_cent
    return (centroid_sums, gram_sum / tokens_all)


def solution(mesh):
    in_specs = (
        P("fsdp", "cent"),
        P("cent", "fsdp"),
        P(("fsdp", "cent"), None),
        P(),
        P("cent", None),
        P(("fsdp", "cent")),
        P("fsdp", None),
    )
    out_specs = (P("cent", "fsdp"), P("fsdp", "cent"))
    return jax.shard_map(shards, mesh=mesh, in_specs=in_specs, out_specs=out_specs, check_vma=False)
```

```python
import functools

import jax
import jax.numpy as jnp
from jax import lax
from jax.experimental import pallas as pl
from jax.experimental.pallas import tpu as pltpu
from jax.sharding import PartitionSpec as P

TILE = 8
LT = 8
NY = 8
NX = 4
MESH = pl.DeviceIdType.MESH


def ring_arrivals(size, sign):
    arrivals = []
    for hops in range(1, size // 2 + 1):
        arrivals.append((hops, -sign * hops, sign, hops < size // 2))
        if hops < size // 2:
            arrivals.append((hops, sign * hops, -sign, hops < size // 2 - 1))
    return arrivals


def chip_order():
    def hops(chip):
        return min(chip[0], NY - chip[0]) + min(chip[1], NX - chip[1])

    return sorted(((dy, dx) for dy in range(NY) for dx in range(NX)), key=lambda c: (hops(c), c))


def plane_device(place, dy, dx, core):
    x = lax.rem(place // 2, NX)
    y = place // (2 * NX)
    return (lax.rem(y + dy + NY, NY) * NX + lax.rem(x + dx + NX, NX)) * 2 + core


def greet(place, me, peers):
    my_core = lax.rem(place, 2)
    barrier = pltpu.get_barrier_semaphore()
    around = [plane_device(place, dy, dx, my_core) for dy, dx in ((1, 0), (-1, 0), (0, 1), (0, -1))]
    around.append(plane_device(place, 0, 0, 1 - my_core))
    for other in around:
        pl.semaphore_signal(barrier, inc=1, device_id=(other, me), device_id_type=MESH)
    for peer in peers:
        pl.semaphore_signal(barrier, inc=1, device_id=(place, peer), device_id_type=MESH)
    pl.semaphore_wait(barrier, len(around) + len(peers))


def plane_walk(core, place, me, block, out, send_sem, recv_sem, own_sem, after=None):
    first_is_y, sign = core == 0, 1 - 2 * core

    def offsets(first, second):
        return (first, second) if first_is_y else (second, first)

    def device_at(dy, dx, which):
        return plane_device(place, dy, dx, which)

    sizes = (NY, NX) if first_is_y else (NX, NY)
    copies = []
    here = {(0, 0, core)}

    def send(source, origin, target):
        copy = pltpu.make_async_remote_copy(
            src_ref=source,
            dst_ref=out.at[origin],
            send_sem=send_sem.at[len(copies)],
            recv_sem=recv_sem.at[origin],
            device_id=(target, me),
            device_id_type=MESH,
        )
        copy.start()
        copies.append(copy)

    def arrive(dy, dx, which):
        if (dy % NY, dx % NX, which) in here:
            return
        here.add((dy % NY, dx % NX, which))
        origin = device_at(dy, dx, which)
        pltpu.make_async_remote_copy(
            src_ref=out.at[origin],
            dst_ref=out.at[origin],
            send_sem=send_sem.at[0],
            recv_sem=recv_sem.at[origin],
            device_id=(device_at(0, 0, 1 - core), me),
            device_id_type=MESH,
        ).wait_recv()

    own = pltpu.make_async_copy(block, out.at[place], own_sem)
    own.start()
    firsts = [(0, 0, 0, False)] + ring_arrivals(sizes[0], sign)
    seconds = ring_arrivals(sizes[1], sign)
    events = []
    for number, (hops, offset, way, goes_on) in enumerate(firsts):
        events.append((hops, 0, number, 0, (offset, 0), way, goes_on))
        for later, (more, across, turn, on_too) in enumerate(seconds):
            events.append((hops + more, 1, number, later, (offset, across), turn, on_too))
    events.sort()
    for at, (hops, leg, unused, also_unused, offset, way, goes_on) in enumerate(events):
        dy, dx = offsets(*offset)
        origin = device_at(dy, dx, core)
        source = block
        if hops > 0:
            arrive(dy, dx, core)
            source = out.at[origin]
        if leg == 0:
            for turn in (1, -1) if hops == 0 else (way,) if goes_on else ():
                send(source, origin, device_at(*offsets(turn, 0), core))
            for turn in (1, -1):
                send(source, origin, device_at(*offsets(0, turn), core))
        elif goes_on:
            send(source, origin, device_at(*offsets(0, way), core))
        send(source, origin, device_at(0, 0, 1 - core))
        if at + 1 == len(events) or events[at + 1][0] > hops:
            if hops == 0:
                own.wait()
            if after is not None:
                after(hops, arrive)
    for dy, dx in chip_order():
        arrive(dy, dx, 1 - core)
    for copy in copies:
        copy.wait_send()


GROUPS = 4


def project_kernel(n, *refs):
    attention, block, tiles, head, tiles_out = refs[:5]
    w_all, stage, landed, send_sem, recv_sem, own_sem, part_send, part_recv = refs[5:13]
    tile_send, tile_recv, tile_own = refs[13:]
    place, me = lax.axis_index("fsdp"), lax.axis_index("cent")
    greet(place, me, [lax.rem(me + step, n) for step in range(1, n)])
    order = chip_order()
    per_group = len(order) // GROUPS
    tok_dev = head.shape[0]

    def part(group, step):
        peer = lax.rem(me + step, n)
        slots = pl.ds(group * per_group, per_group)
        return pltpu.make_async_remote_copy(
            src_ref=stage.at[peer, slots],
            dst_ref=landed.at[step, slots],
            send_sem=part_send.at[group, step],
            recv_sem=part_recv.at[group, step],
            device_id=(place, peer),
            device_id_type=MESH,
        )

    def tile(source, origin, offset, way):
        return pltpu.make_async_remote_copy(
            src_ref=source,
            dst_ref=tiles_out.at[origin],
            send_sem=tile_send.at[(offset - way) % n],
            recv_sem=tile_recv.at[(offset - way) % n],
            device_id=(place, lax.rem(me + way + n, n)),
            device_id_type=MESH,
        )

    def run(core):
        turns = ring_arrivals(n, 1 - 2 * core) if n > 2 else [(1, 1, -1, False)]
        sent = []

        def pass_tiles(hops):
            if hops == 0:
                for way in (1, -1) if n > 2 else (1,):
                    copy = tile(tiles, me, 0, way)
                    copy.start()
                    sent.append(copy)
            for steps, offset, way, goes_on in turns:
                if steps == hops:
                    origin = lax.rem(me + offset + n, n)
                    tile(tiles_out.at[origin], origin, offset + way, way).wait_recv()
                    if goes_on:
                        copy = tile(tiles_out.at[origin], origin, offset, way)
                        copy.start()
                        sent.append(copy)

        def multiply(group, arrive):
            rows = attention[...]
            for slot in range(group * per_group, (group + 1) * per_group):
                dy, dx = order[slot]
                arrive(dy, dx, 0)
                arrive(dy, dx, 1)
                both = w_all[pl.ds(plane_device(place, dy, dx, 0), 2)]
                columns = lax.dot_general(
                    rows,
                    both.reshape(2 * both.shape[1], both.shape[2]),
                    (((1,), (1,)), ((), ())),
                    preferred_element_type=jnp.float32,
                ).astype(jnp.bfloat16)
                stage[:, slot] = columns.reshape(n, tok_dev, columns.shape[1])
            for step in sorted(range(1, n), key=lambda s: -min(s, n - s)):
                part(group, step).start()

        def after(hops, arrive):
            pass_tiles(hops)
            if 3 <= hops <= 5:
                multiply(hops - 3, arrive)
            elif hops == 6:
                multiply(3, arrive)

        plane_walk(core, place, me, block, w_all, send_sem, recv_sem, own_sem, after)
        for copy in sent:
            copy.wait_send()

    for core in range(2):

        @pl.when(lax.rem(place, 2) == core)
        def _():
            run(core)

    own = pltpu.make_async_copy(tiles, tiles_out.at[me], tile_own)
    own.start()
    for group in range(GROUPS):
        for step in range(1, n):
            part(group, step).wait()
        for slot in range(group * per_group, (group + 1) * per_group):
            total = stage[me, slot].astype(jnp.float32)
            for step in range(1, n):
                total = total + landed[step, slot].astype(jnp.float32)
            dy, dx = order[slot]
            start = pl.multiple_of(plane_device(place, dy, dx, 0) // 2 * 128, 128)
            head[:, pl.ds(start, 128)] = total
    own.wait()


def project(n, collective_id, attention, block, tiles):
    devices = NY * NX * 2
    tok_dev = attention.shape[0] // n
    chips = NY * NX
    wide = 2 * block.shape[0]
    pieces = pltpu.VMEM((n, chips, tok_dev, wide), jnp.bfloat16)
    return pl.pallas_call(
        functools.partial(project_kernel, n),
        out_shape=[
            jax.ShapeDtypeStruct((tok_dev, chips * wide), jnp.float32),
            jax.ShapeDtypeStruct((n,) + tiles.shape, tiles.dtype),
        ],
        in_specs=[pl.BlockSpec(memory_space=pltpu.VMEM)] * 3,
        out_specs=[pl.BlockSpec(memory_space=pltpu.VMEM)] * 2,
        scratch_shapes=[
            pltpu.VMEM((devices,) + block.shape, block.dtype),
            pieces,
            pieces,
            pltpu.SemaphoreType.DMA((devices,)),
            pltpu.SemaphoreType.DMA((devices,)),
            pltpu.SemaphoreType.DMA,
            pltpu.SemaphoreType.DMA((GROUPS, n)),
            pltpu.SemaphoreType.DMA((GROUPS, n)),
            pltpu.SemaphoreType.DMA((n,)),
            pltpu.SemaphoreType.DMA((n,)),
            pltpu.SemaphoreType.DMA,
        ],
        compiler_params=pltpu.CompilerParams(
            collective_id=collective_id, has_side_effects=True, vmem_limit_bytes=32 * 1024 * 1024
        ),
    )(attention, block, tiles)


def moments_kernel(n, tokens, *refs):
    block, sums, gram, rows, gram_out, gram_in, sums_out, sums_in = refs[:8]
    send_sem, recv_sem, own_sem, gram_send, gram_recv, sums_send, sums_recv = refs[8:]
    place, me = lax.axis_index("fsdp"), lax.axis_index("cent")
    greet(place, me, [lax.rem(me + step, n) for step in range(1, n)])
    rows_dev, cols_dev = gram.shape
    cent_dev = sums.shape[0]
    feat_dim = n * cols_dev
    count = rows.shape[0] * rows.shape[1]
    far_first = sorted(range(1, n), key=lambda s: -min(s, n - s))

    def part(step, source, target, sent, got):
        peer = lax.rem(me + step, n)
        return pltpu.make_async_remote_copy(
            src_ref=source.at[peer],
            dst_ref=target.at[step],
            send_sem=sent.at[step],
            recv_sem=got.at[step],
            device_id=(place, peer),
            device_id_type=MESH,
        )

    def gram_part(step):
        return part(step, gram_out, gram_in, gram_send, gram_recv)

    def sums_part(step):
        return part(step, sums_out, sums_in, sums_send, sums_recv)

    def run(core):
        plane_walk(core, place, me, block, rows, send_sem, recv_sem, own_sem)
        pair = rows[:, :, pl.ds(pl.multiple_of(place // 2 * 128, 128), 128)].reshape(count, 128)
        half = slice(rows_dev * core, rows_dev * (core + 1))
        left = pair.T[half]
        for step in far_first + [0]:
            peer = lax.rem(me + step, n)
            right = rows[:, :, pl.ds(pl.multiple_of(peer * cols_dev, cols_dev), cols_dev)]
            gram_out[peer] = jnp.dot(
                left, right.reshape(count, cols_dev), preferred_element_type=jnp.float32
            ).astype(jnp.bfloat16)
            if step > 0:
                gram_part(step).start()
        label = rows[:, :, feat_dim:].reshape(count, 128).T[:8].astype(jnp.float32)
        cent_id = label[0:1] * TILE + label[1:2]
        number = lax.broadcasted_iota(jnp.int32, (n * cent_dev, count), 0).astype(jnp.float32)
        onehot = jnp.where(number == cent_id, 1.0, 0.0).astype(jnp.bfloat16)
        both = jnp.dot(onehot, pair, preferred_element_type=jnp.float32)
        sums_out[...] = both[:, half].astype(jnp.bfloat16).reshape(n, cent_dev, rows_dev)
        for step in far_first:
            sums_part(step).start()

    for core in range(2):

        @pl.when(lax.rem(place, 2) == core)
        def _():
            run(core)

    total = gram_out[me].astype(jnp.float32)
    for step in range(1, n):
        gram_part(step).wait()
        total = total + gram_in[step].astype(jnp.float32)
    gram[...] = total * (1.0 / tokens)
    total = sums_out[me].astype(jnp.float32)
    for step in range(1, n):
        sums_part(step).wait()
        total = total + sums_in[step].astype(jnp.float32)
    sums[...] = total


def moments(n, collective_id, block, feat_dim, cent_dev):
    devices = NY * NX * 2
    rows_dev, cols_dev = feat_dim // devices, feat_dim // n
    tokens = block.shape[0] * devices * n
    gram_pieces = pltpu.VMEM((n, rows_dev, cols_dev), jnp.bfloat16)
    sums_pieces = pltpu.VMEM((n, cent_dev, rows_dev), jnp.bfloat16)
    return pl.pallas_call(
        functools.partial(moments_kernel, n, tokens),
        out_shape=[
            jax.ShapeDtypeStruct((cent_dev, rows_dev), jnp.float32),
            jax.ShapeDtypeStruct((rows_dev, cols_dev), jnp.float32),
        ],
        in_specs=[pl.BlockSpec(memory_space=pltpu.VMEM)],
        out_specs=[pl.BlockSpec(memory_space=pltpu.VMEM)] * 2,
        scratch_shapes=[
            pltpu.VMEM((devices,) + block.shape, block.dtype),
            gram_pieces,
            gram_pieces,
            sums_pieces,
            sums_pieces,
            pltpu.SemaphoreType.DMA((devices,)),
            pltpu.SemaphoreType.DMA((devices,)),
            pltpu.SemaphoreType.DMA,
            pltpu.SemaphoreType.DMA((n,)),
            pltpu.SemaphoreType.DMA((n,)),
            pltpu.SemaphoreType.DMA((n,)),
            pltpu.SemaphoreType.DMA((n,)),
        ],
        compiler_params=pltpu.CompilerParams(
            collective_id=collective_id, has_side_effects=True, vmem_limit_bytes=48 * 1024 * 1024
        ),
    )(block)


def shards(attention, w_out, hidden, norm_gain, centroids, token_codes, tile_lists):
    tok_dev = hidden.shape[0]
    feat_dim = hidden.shape[1]
    n_cent = lax.axis_size("cent")
    cap_slots = max(2, 2 * LT // n_cent)
    cent_dev = centroids.shape[0]
    own_tiles = cent_dev // TILE
    owner_idx = lax.axis_index("cent")
    listed = tile_lists[0]
    local_tile = listed - owner_idx * own_tiles
    owned_here = (local_tile >= 0) & (local_tile < own_tiles)
    safe_tile = jnp.clip(local_tile, 0, own_tiles - 1)
    tiles_here = centroids.reshape(own_tiles, TILE, feat_dim)
    slot_of = token_codes // TILE
    offset = token_codes % TILE
    list_pos = jnp.arange(LT, dtype=jnp.int32)
    owner_of = listed // own_tiles
    earlier = (owner_of[None, :] == owner_of[:, None]) & (list_pos[None, :] < list_pos[:, None])
    rank_all = jnp.sum(earlier.astype(jnp.int32), axis=1)
    chosen = owned_here[None, :] & (
        rank_all[None, :] == jnp.arange(cap_slots, dtype=jnp.int32)[:, None]
    )
    send_tile = jnp.sum(jnp.where(chosen, safe_tile[None, :], 0), axis=1)
    outgoing = jnp.take(tiles_here, send_tile, axis=0).reshape(cap_slots * TILE, feat_dim)
    head_sum, arrived = project(n_cent, 0, attention, w_out.T, outgoing)
    where_tile = owner_of * cap_slots + rank_all
    tile_rows = arrived.reshape(-1, feat_dim)
    centers = jnp.take(tile_rows, where_tile[slot_of] * TILE + offset, axis=0)
    tile_of = listed[slot_of]

    mixed_rows = hidden.astype(jnp.float32) + head_sum
    normed = (
        mixed_rows
        * lax.rsqrt(jnp.mean(mixed_rows * mixed_rows, axis=1, keepdims=True) + 1e-05)
        * norm_gain.astype(jnp.float32)
    )
    residual = (normed - centers.astype(jnp.float32)).astype(jnp.bfloat16)

    lane = jnp.arange(128, dtype=jnp.int32)[None, :]
    label = jnp.where(
        lane == 0, tile_of[:, None], jnp.where(lane == 1, offset[:, None], 0)
    ).astype(jnp.bfloat16)
    return tuple(
        moments(n_cent, 1, jnp.concatenate([residual, label], axis=1), feat_dim, cent_dev)
    )


def solution(mesh):
    in_specs = (
        P("fsdp", "cent"),
        P("cent", "fsdp"),
        P(("fsdp", "cent"), None),
        P(),
        P("cent", None),
        P(("fsdp", "cent")),
        P("fsdp", None),
    )
    out_specs = (P("cent", "fsdp"), P("fsdp", "cent"))
    return jax.shard_map(shards, mesh=mesh, in_specs=in_specs, out_specs=out_specs, check_vma=False)
```

```python
import functools

import jax
import jax.numpy as jnp
from jax import lax
from jax.experimental import pallas as pl
from jax.experimental.pallas import tpu as pltpu
from jax.sharding import PartitionSpec as P

TILE = 8
LT = 8
NY = 8
NX = 4
MESH = pl.DeviceIdType.MESH


def ring_arrivals(size, sign):
    arrivals = []
    for hops in range(1, size // 2 + 1):
        arrivals.append((hops, -sign * hops, sign, hops < size // 2))
        if hops < size // 2:
            arrivals.append((hops, sign * hops, -sign, hops < size // 2 - 1))
    return arrivals


def chip_order():
    def hops(chip):
        return min(chip[0], NY - chip[0]) + min(chip[1], NX - chip[1])

    return sorted(((dy, dx) for dy in range(NY) for dx in range(NX)), key=lambda c: (hops(c), c))


def plane_device(place, dy, dx, core):
    x = lax.rem(place // 2, NX)
    y = place // (2 * NX)
    return (lax.rem(y + dy + NY, NY) * NX + lax.rem(x + dx + NX, NX)) * 2 + core


def greet(place, me, peers):
    my_core = lax.rem(place, 2)
    barrier = pltpu.get_barrier_semaphore()
    around = [plane_device(place, dy, dx, my_core) for dy, dx in ((1, 0), (-1, 0), (0, 1), (0, -1))]
    around.append(plane_device(place, 0, 0, 1 - my_core))
    for other in around:
        pl.semaphore_signal(barrier, inc=1, device_id=(other, me), device_id_type=MESH)
    for peer in peers:
        pl.semaphore_signal(barrier, inc=1, device_id=(place, peer), device_id_type=MESH)
    pl.semaphore_wait(barrier, len(around) + len(peers))


def plane_walk(core, place, me, block, out, send_sem, recv_sem, own_sem, after=None):
    first_is_y, sign = core == 0, 1 - 2 * core

    def offsets(first, second):
        return (first, second) if first_is_y else (second, first)

    def device_at(dy, dx, which):
        return plane_device(place, dy, dx, which)

    sizes = (NY, NX) if first_is_y else (NX, NY)
    copies = []
    here = {(0, 0, core)}

    def send(source, origin, target):
        copy = pltpu.make_async_remote_copy(
            src_ref=source,
            dst_ref=out.at[origin],
            send_sem=send_sem.at[len(copies)],
            recv_sem=recv_sem.at[origin],
            device_id=(target, me),
            device_id_type=MESH,
        )
        copy.start()
        copies.append(copy)

    def arrive(dy, dx, which):
        if (dy % NY, dx % NX, which) in here:
            return
        here.add((dy % NY, dx % NX, which))
        origin = device_at(dy, dx, which)
        pltpu.make_async_remote_copy(
            src_ref=out.at[origin],
            dst_ref=out.at[origin],
            send_sem=send_sem.at[0],
            recv_sem=recv_sem.at[origin],
            device_id=(device_at(0, 0, 1 - core), me),
            device_id_type=MESH,
        ).wait_recv()

    own = pltpu.make_async_copy(block, out.at[place], own_sem)
    own.start()
    firsts = [(0, 0, 0, False)] + ring_arrivals(sizes[0], sign)
    seconds = ring_arrivals(sizes[1], sign)
    events = []
    for number, (hops, offset, way, goes_on) in enumerate(firsts):
        events.append((hops, 0, number, 0, (offset, 0), way, goes_on))
        for later, (more, across, turn, on_too) in enumerate(seconds):
            events.append((hops + more, 1, number, later, (offset, across), turn, on_too))
    events.sort()
    for at, (hops, leg, unused, also_unused, offset, way, goes_on) in enumerate(events):
        dy, dx = offsets(*offset)
        origin = device_at(dy, dx, core)
        source = block
        if hops > 0:
            arrive(dy, dx, core)
            source = out.at[origin]
        if leg == 0:
            for turn in (1, -1) if hops == 0 else (way,) if goes_on else ():
                send(source, origin, device_at(*offsets(turn, 0), core))
            for turn in (1, -1):
                send(source, origin, device_at(*offsets(0, turn), core))
        elif goes_on:
            send(source, origin, device_at(*offsets(0, way), core))
        send(source, origin, device_at(0, 0, 1 - core))
        if at + 1 == len(events) or events[at + 1][0] > hops:
            if hops == 0:
                own.wait()
            if after is not None:
                after(hops, arrive)
    for dy, dx in chip_order():
        arrive(dy, dx, 1 - core)
    for copy in copies:
        copy.wait_send()


GROUPS = 4


def project_kernel(n, *refs):
    attention, block, tiles, head, tiles_out = refs[:5]
    w_all, stage, landed, send_sem, recv_sem, own_sem, part_send, part_recv = refs[5:13]
    tile_send, tile_recv, tile_own = refs[13:]
    place, me = lax.axis_index("fsdp"), lax.axis_index("cent")
    greet(place, me, [lax.rem(me + step, n) for step in range(1, n)])
    order = chip_order()
    per_group = len(order) // GROUPS
    tok_dev = head.shape[0]

    def part(group, step):
        peer = lax.rem(me + step, n)
        slots = pl.ds(group * per_group, per_group)
        return pltpu.make_async_remote_copy(
            src_ref=stage.at[peer, slots],
            dst_ref=landed.at[step, slots],
            send_sem=part_send.at[group, step],
            recv_sem=part_recv.at[group, step],
            device_id=(place, peer),
            device_id_type=MESH,
        )

    def tile(source, origin, offset, way):
        return pltpu.make_async_remote_copy(
            src_ref=source,
            dst_ref=tiles_out.at[origin],
            send_sem=tile_send.at[(offset - way) % n],
            recv_sem=tile_recv.at[(offset - way) % n],
            device_id=(place, lax.rem(me + way + n, n)),
            device_id_type=MESH,
        )

    def run(core):
        turns = ring_arrivals(n, 1 - 2 * core) if n > 2 else [(1, 1, -1, False)]
        sent = []

        def pass_tiles(hops):
            if hops == 0:
                for way in (1, -1) if n > 2 else (1,):
                    copy = tile(tiles, me, 0, way)
                    copy.start()
                    sent.append(copy)
            for steps, offset, way, goes_on in turns:
                if steps == hops:
                    origin = lax.rem(me + offset + n, n)
                    tile(tiles_out.at[origin], origin, offset + way, way).wait_recv()
                    if goes_on:
                        copy = tile(tiles_out.at[origin], origin, offset, way)
                        copy.start()
                        sent.append(copy)

        def multiply(group, arrive):
            rows = attention[...]
            for slot in range(group * per_group, (group + 1) * per_group):
                dy, dx = order[slot]
                arrive(dy, dx, 0)
                arrive(dy, dx, 1)
                both = w_all[pl.ds(plane_device(place, dy, dx, 0), 2)]
                columns = lax.dot_general(
                    rows,
                    both.reshape(2 * both.shape[1], both.shape[2]),
                    (((1,), (1,)), ((), ())),
                    preferred_element_type=jnp.float32,
                ).astype(jnp.bfloat16)
                stage[:, slot] = columns.reshape(n, tok_dev, columns.shape[1])
            for step in sorted(range(1, n), key=lambda s: -min(s, n - s)):
                part(group, step).start()

        def after(hops, arrive):
            pass_tiles(hops)
            if 2 <= hops <= 4:
                multiply(hops - 2, arrive)
            elif hops == 6:
                multiply(3, arrive)

        plane_walk(core, place, me, block, w_all, send_sem, recv_sem, own_sem, after)
        for copy in sent:
            copy.wait_send()

    for core in range(2):

        @pl.when(lax.rem(place, 2) == core)
        def _():
            run(core)

    own = pltpu.make_async_copy(tiles, tiles_out.at[me], tile_own)
    own.start()
    for group in range(GROUPS):
        for step in range(1, n):
            part(group, step).wait()
        for slot in range(group * per_group, (group + 1) * per_group):
            total = stage[me, slot].astype(jnp.float32)
            for step in range(1, n):
                total = total + landed[step, slot].astype(jnp.float32)
            dy, dx = order[slot]
            start = pl.multiple_of(plane_device(place, dy, dx, 0) // 2 * 128, 128)
            head[:, pl.ds(start, 128)] = total
    own.wait()


def project(n, collective_id, attention, block, tiles):
    devices = NY * NX * 2
    tok_dev = attention.shape[0] // n
    chips = NY * NX
    wide = 2 * block.shape[0]
    pieces = pltpu.VMEM((n, chips, tok_dev, wide), jnp.bfloat16)
    return pl.pallas_call(
        functools.partial(project_kernel, n),
        out_shape=[
            jax.ShapeDtypeStruct((tok_dev, chips * wide), jnp.float32),
            jax.ShapeDtypeStruct((n,) + tiles.shape, tiles.dtype),
        ],
        in_specs=[pl.BlockSpec(memory_space=pltpu.VMEM)] * 3,
        out_specs=[pl.BlockSpec(memory_space=pltpu.VMEM)] * 2,
        scratch_shapes=[
            pltpu.VMEM((devices,) + block.shape, block.dtype),
            pieces,
            pieces,
            pltpu.SemaphoreType.DMA((devices,)),
            pltpu.SemaphoreType.DMA((devices,)),
            pltpu.SemaphoreType.DMA,
            pltpu.SemaphoreType.DMA((GROUPS, n)),
            pltpu.SemaphoreType.DMA((GROUPS, n)),
            pltpu.SemaphoreType.DMA((n,)),
            pltpu.SemaphoreType.DMA((n,)),
            pltpu.SemaphoreType.DMA,
        ],
        compiler_params=pltpu.CompilerParams(
            collective_id=collective_id, has_side_effects=True, vmem_limit_bytes=32 * 1024 * 1024
        ),
    )(attention, block, tiles)


def moments_kernel(n, tokens, *refs):
    block, sums, gram, rows, gram_out, gram_in, sums_out, sums_in = refs[:8]
    send_sem, recv_sem, own_sem, gram_send, gram_recv, sums_send, sums_recv = refs[8:]
    place, me = lax.axis_index("fsdp"), lax.axis_index("cent")
    greet(place, me, [lax.rem(me + step, n) for step in range(1, n)])
    rows_dev, cols_dev = gram.shape
    cent_dev = sums.shape[0]
    feat_dim = n * cols_dev
    count = rows.shape[0] * rows.shape[1]
    far_first = sorted(range(1, n), key=lambda s: -min(s, n - s))

    def part(step, source, target, sent, got):
        peer = lax.rem(me + step, n)
        return pltpu.make_async_remote_copy(
            src_ref=source.at[peer],
            dst_ref=target.at[step],
            send_sem=sent.at[step],
            recv_sem=got.at[step],
            device_id=(place, peer),
            device_id_type=MESH,
        )

    def gram_part(step):
        return part(step, gram_out, gram_in, gram_send, gram_recv)

    def sums_part(step):
        return part(step, sums_out, sums_in, sums_send, sums_recv)

    def run(core):
        plane_walk(core, place, me, block, rows, send_sem, recv_sem, own_sem)
        pair = rows[:, :, pl.ds(pl.multiple_of(place // 2 * 128, 128), 128)].reshape(count, 128)
        half = slice(rows_dev * core, rows_dev * (core + 1))
        left = pair.T[half]
        for step in far_first + [0]:
            peer = lax.rem(me + step, n)
            right = rows[:, :, pl.ds(pl.multiple_of(peer * cols_dev, cols_dev), cols_dev)]
            gram_out[peer] = jnp.dot(
                left, right.reshape(count, cols_dev), preferred_element_type=jnp.float32
            ).astype(jnp.bfloat16)
            if step > 0:
                gram_part(step).start()
        label = rows[:, :, feat_dim:].reshape(count, 128).T[:8].astype(jnp.float32)
        cent_id = label[0:1] * TILE + label[1:2]
        number = lax.broadcasted_iota(jnp.int32, (n * cent_dev, count), 0).astype(jnp.float32)
        onehot = jnp.where(number == cent_id, 1.0, 0.0).astype(jnp.bfloat16)
        both = jnp.dot(onehot, pair, preferred_element_type=jnp.float32)
        sums_out[...] = both[:, half].astype(jnp.bfloat16).reshape(n, cent_dev, rows_dev)
        for step in far_first:
            sums_part(step).start()

    for core in range(2):

        @pl.when(lax.rem(place, 2) == core)
        def _():
            run(core)

    total = gram_out[me].astype(jnp.float32)
    for step in range(1, n):
        gram_part(step).wait()
        total = total + gram_in[step].astype(jnp.float32)
    gram[...] = total * (1.0 / tokens)
    total = sums_out[me].astype(jnp.float32)
    for step in range(1, n):
        sums_part(step).wait()
        total = total + sums_in[step].astype(jnp.float32)
    sums[...] = total


def moments(n, collective_id, block, feat_dim, cent_dev):
    devices = NY * NX * 2
    rows_dev, cols_dev = feat_dim // devices, feat_dim // n
    tokens = block.shape[0] * devices * n
    gram_pieces = pltpu.VMEM((n, rows_dev, cols_dev), jnp.bfloat16)
    sums_pieces = pltpu.VMEM((n, cent_dev, rows_dev), jnp.bfloat16)
    return pl.pallas_call(
        functools.partial(moments_kernel, n, tokens),
        out_shape=[
            jax.ShapeDtypeStruct((cent_dev, rows_dev), jnp.float32),
            jax.ShapeDtypeStruct((rows_dev, cols_dev), jnp.float32),
        ],
        in_specs=[pl.BlockSpec(memory_space=pltpu.VMEM)],
        out_specs=[pl.BlockSpec(memory_space=pltpu.VMEM)] * 2,
        scratch_shapes=[
            pltpu.VMEM((devices,) + block.shape, block.dtype),
            gram_pieces,
            gram_pieces,
            sums_pieces,
            sums_pieces,
            pltpu.SemaphoreType.DMA((devices,)),
            pltpu.SemaphoreType.DMA((devices,)),
            pltpu.SemaphoreType.DMA,
            pltpu.SemaphoreType.DMA((n,)),
            pltpu.SemaphoreType.DMA((n,)),
            pltpu.SemaphoreType.DMA((n,)),
            pltpu.SemaphoreType.DMA((n,)),
        ],
        compiler_params=pltpu.CompilerParams(
            collective_id=collective_id, has_side_effects=True, vmem_limit_bytes=48 * 1024 * 1024
        ),
    )(block)


def shards(attention, w_out, hidden, norm_gain, centroids, token_codes, tile_lists):
    tok_dev = hidden.shape[0]
    feat_dim = hidden.shape[1]
    n_cent = lax.axis_size("cent")
    cap_slots = max(2, 2 * LT // n_cent)
    cent_dev = centroids.shape[0]
    own_tiles = cent_dev // TILE
    owner_idx = lax.axis_index("cent")
    listed = tile_lists[0]
    local_tile = listed - owner_idx * own_tiles
    owned_here = (local_tile >= 0) & (local_tile < own_tiles)
    safe_tile = jnp.clip(local_tile, 0, own_tiles - 1)
    tiles_here = centroids.reshape(own_tiles, TILE, feat_dim)
    slot_of = token_codes // TILE
    offset = token_codes % TILE
    list_pos = jnp.arange(LT, dtype=jnp.int32)
    owner_of = listed // own_tiles
    earlier = (owner_of[None, :] == owner_of[:, None]) & (list_pos[None, :] < list_pos[:, None])
    rank_all = jnp.sum(earlier.astype(jnp.int32), axis=1)
    chosen = owned_here[None, :] & (
        rank_all[None, :] == jnp.arange(cap_slots, dtype=jnp.int32)[:, None]
    )
    send_tile = jnp.sum(jnp.where(chosen, safe_tile[None, :], 0), axis=1)
    outgoing = jnp.take(tiles_here, send_tile, axis=0).reshape(cap_slots * TILE, feat_dim)
    head_sum, arrived = project(n_cent, 0, attention, w_out.T, outgoing)
    where_tile = owner_of * cap_slots + rank_all
    tile_rows = arrived.reshape(-1, feat_dim)
    centers = jnp.take(tile_rows, where_tile[slot_of] * TILE + offset, axis=0)
    tile_of = listed[slot_of]

    mixed_rows = hidden.astype(jnp.float32) + head_sum
    normed = (
        mixed_rows
        * lax.rsqrt(jnp.mean(mixed_rows * mixed_rows, axis=1, keepdims=True) + 1e-05)
        * norm_gain.astype(jnp.float32)
    )
    residual = (normed - centers.astype(jnp.float32)).astype(jnp.bfloat16)

    lane = jnp.arange(128, dtype=jnp.int32)[None, :]
    label = jnp.where(
        lane == 0, tile_of[:, None], jnp.where(lane == 1, offset[:, None], 0)
    ).astype(jnp.bfloat16)
    return tuple(
        moments(n_cent, 1, jnp.concatenate([residual, label], axis=1), feat_dim, cent_dev)
    )


def solution(mesh):
    in_specs = (
        P("fsdp", "cent"),
        P("cent", "fsdp"),
        P(("fsdp", "cent"), None),
        P(),
        P("cent", None),
        P(("fsdp", "cent")),
        P("fsdp", None),
    )
    out_specs = (P("cent", "fsdp"), P("fsdp", "cent"))
    return jax.shard_map(shards, mesh=mesh, in_specs=in_specs, out_specs=out_specs, check_vma=False)
```
